32 devices in a mesh: bins: 16 (over z, y, x), params: 2 (over core).
Axes of the slice: x: 2, y: 2, z: 4, core: 2. Of those that a mesh axis runs over, the one named last changes fastest.
Arguments:
- event_bins: int32 [49152], P('bins'), may hold values from 0 to 16383, as said below
- event_weights: bfloat16 [49152, 3072], P('bins', 'params'), may hold values from -6 to 6
- nominal: bfloat16 [49152], P('bins'), may hold values from 0.5 to 2
- background: float32 [16384], P('bins'), may hold values from 1 to 10
- observed: float32 [16384], P('bins'), may hold values from 1 to 100
Outputs:
- hessian: float32 [3072, 3072], P(('params', 'bins'))
The draws below stay inside these ranges and needn't reach their ends.
Inputs may be any that keep to these rules, and one draw needn't show every extreme that they name: `event_bins`: each index of bins holds 3072 consecutive events in ascending bin order. The owner of bin b is b // 1024; each owner's bins receive from one index of bins between 96 and 288 of its events, and in every draw every index of bins has some owner that receives exactly 288 of its events.
All inputs are finite; a program needn't handle non-finite values.
Results may differ from the reference program's by a relative error of at most 0.0016.
Values may be sent and summed in bfloat16 or wider, within the bound.
A program may use at most 128 MiB of HBM per device.

```python
import math
import jax
import jax.numpy as jnp
from jax import lax

P_SIZE = 3072
BINS_DEV = 1024
E_DEV = 3072
PG = 1536
NB = 16384
EVENTS = 49152
COLS = 3072
N_BINS = 16
N_PARAMS = 2


def draw_event_bins(key, part):
    base_count = E_DEV // N_BINS
    swing_most = base_count // 2

    def one_source(subkey):
        key_swing, key_perm, key_bins = jax.random.split(subkey, 3)
        swing = jax.random.randint(key_swing, (N_BINS // 2,), -swing_most, swing_most + 1)
        swing = swing.at[0].set(swing_most)
        profile = jnp.concatenate([base_count + swing, base_count - swing])
        counts = profile[jax.random.permutation(key_perm, N_BINS)]
        bounds = jnp.cumsum(counts)
        ordinal = jnp.arange(E_DEV, dtype=jnp.int32)
        target = jnp.sum((bounds[None, :] <= ordinal[:, None]).astype(jnp.int32), axis=1)
        inside = jax.random.randint(key_bins, (E_DEV,), 0, BINS_DEV)
        return jnp.sort(target * BINS_DEV + inside).astype(jnp.int32)
    source_keys = jax.random.split(jax.random.fold_in(key, 7), N_BINS)
    return jax.vmap(one_source)(source_keys).reshape(-1)


def steps_of(stream_key, shape, pieces, least, top_value):
    factor_of = 1.0
    for dim, parts in pieces:
        draws = jax.random.uniform(jax.random.fold_in(jax.random.fold_in(stream_key, 6), dim), (parts,), jnp.float32, least / len(pieces), top_value / len(pieces))
        factor_of = factor_of * jnp.repeat(jnp.exp(draws), shape[dim] // parts).reshape((-1,) + (1,) * (len(shape) - 1 - dim))
    return factor_of


def gaussian(key, extent, scale, limit, cuts=(), kind=jnp.bfloat16):
    result = scale * jax.random.normal(key, extent, jnp.float32)
    if cuts:
        result = result * steps_of(key, extent, cuts, -0.22, 0.18)
    return jnp.clip(result, -limit, limit).astype(kind)


def setup_inputs(seed: int = 0) -> dict:
    keys = jax.random.split(jax.random.key(seed), 6)
    return {
        "event_bins": draw_event_bins(jax.random.fold_in(keys[5], 71), 0),
        "event_weights": gaussian(keys[1], (EVENTS, P_SIZE), 1.0, 6.0, ((0, 16), (1, 2))),
        "nominal": jnp.clip(jnp.exp(math.log(2.0) - 1.3862944 * jax.random.uniform(keys[2], (EVENTS,), jnp.float32) ** steps_of(keys[2], (EVENTS,), ((0, 16),), -0.2, 0.2)), 0.5, 2.0).astype(jnp.bfloat16),
        "background": jnp.clip(jnp.exp(math.log(10.0) - 2.3025851 * jax.random.uniform(keys[3], (NB,), jnp.float32) ** steps_of(keys[3], (NB,), ((0, 16),), -0.2, 0.2)), 1.0, 10.0),
        "observed": jnp.clip(jnp.exp(math.log(100.0) - 4.6051702 * jax.random.uniform(keys[4], (NB,), jnp.float32) ** steps_of(keys[4], (NB,), ((0, 16),), -0.2, 0.2)), 1.0, 100.0),
    }


def reference(event_bins, event_weights, nominal, background, observed):
    bins_split = event_bins.reshape(N_BINS, E_DEV)
    weights_split = event_weights.reshape(N_BINS, E_DEV, P_SIZE)

    def add_source(carry, stacked):
        source_bins, source_weights = stacked
        part_sum = jax.ops.segment_sum(source_weights.astype(jnp.float32), source_bins, num_segments=NB)
        return carry + part_sum, None

    histogram, _ = lax.scan(add_source, jnp.zeros((NB, P_SIZE), jnp.float32), (bins_split, weights_split))
    templates = histogram.astype(jnp.bfloat16)
    nominal_sum = jax.ops.segment_sum(nominal.astype(jnp.float32), event_bins, num_segments=NB)
    yields = background + nominal_sum
    curvature = observed / (yields * yields)
    weighted = (curvature[:, None] * templates.astype(jnp.float32)).astype(jnp.bfloat16)
    dims = (((0,), (0,)), ((), ()))
    full = lax.dot_general(weighted, templates, dims, preferred_element_type=jnp.float32)
    full = full * (1.0 / NB)
    blocks = full.reshape(N_PARAMS, PG, N_PARAMS, PG)
    groups = jnp.arange(N_PARAMS, dtype=jnp.int32)
    tiles = []
    for offset in range(N_PARAMS // 2 + 1):
        tiles.append(blocks[groups, :, (groups + offset) % N_PARAMS, :])
    stacked_tiles = jnp.stack(tiles, axis=2)
    return stacked_tiles.reshape(P_SIZE, COLS)
```

```python
import functools
import math

import jax
import jax.numpy as jnp
from jax import lax
from jax.experimental import pallas as pl
from jax.experimental.pallas import tpu as pltpu
from jax.sharding import PartitionSpec as P

ALIGN = 8


def from_behind(value, axis, steps):
    count = lax.axis_size(axis)
    pairs = [(source, (source + steps) % count) for source in range(count)]
    return lax.ppermute(value, axis, pairs)


def pack_kernel(owners, slot, first, width, starts_ref, rows_ref, out_ref, held, in_sems, out_sems):
    def fetch(o):
        start = pl.multiple_of(starts_ref[o] * ALIGN, ALIGN)
        return pltpu.make_async_copy(
            rows_ref.at[pl.ds(start, slot), pl.ds(first, width)], held.at[o], in_sems.at[o]
        )

    def store(o):
        return pltpu.make_async_copy(held.at[o], out_ref.at[o], out_sems.at[o])

    @pl.loop(0, owners)
    def _(o):
        fetch(o).start()

    @pl.loop(0, owners)
    def _(o):
        fetch(o).wait()
        store(o).start()

    @pl.loop(0, owners)
    def _(o):
        store(o).wait()


def pack(starts, rows, slot, first, width):
    owners = starts.shape[0]
    return pl.pallas_call(
        functools.partial(pack_kernel, owners, slot, first, width),
        out_shape=jax.ShapeDtypeStruct((owners, slot, width), rows.dtype),
        in_specs=[
            pl.BlockSpec(memory_space=pltpu.SMEM),
            pl.BlockSpec(memory_space=pl.ANY),
        ],
        out_specs=pl.BlockSpec(memory_space=pl.ANY),
        scratch_shapes=[
            pltpu.VMEM((owners, slot, width), rows.dtype),
            pltpu.SemaphoreType.DMA((owners,)),
            pltpu.SemaphoreType.DMA((owners,)),
        ],
        compiler_params=pltpu.CompilerParams(vmem_limit_bytes=32 << 20),
        cost_estimate=pl.CostEstimate(
            flops=0, bytes_accessed=4 * owners * slot * width, transcendentals=0
        ),
        name="pack",
    )(starts, rows)


def meta_kernel(bins_dev, starts_ref, table_ref, out_ref):
    owners, _, slot = out_ref.shape
    events = table_ref.shape[1]
    table = table_ref[...]

    @pl.loop(0, owners)
    def _(o):
        start = starts_ref[o] * ALIGN
        turned = pltpu.roll(table, lax.rem(events - start, events), axis=1)[:, :slot]
        bins = turned[0:1] - (o * bins_dev).astype(jnp.float32)
        inside = (bins >= 0) & (bins < bins_dev)
        out_ref[o, 0:1, :] = jnp.where(inside, bins, -1.0)
        out_ref[o, 1:2, :] = turned[1:2]


def pack_meta(starts, table, slot, bins_dev):
    owners = starts.shape[0]
    return pl.pallas_call(
        functools.partial(meta_kernel, bins_dev),
        out_shape=jax.ShapeDtypeStruct((owners, 2, slot), jnp.float32),
        in_specs=[
            pl.BlockSpec(memory_space=pltpu.SMEM),
            pl.BlockSpec(memory_space=pltpu.VMEM),
        ],
        out_specs=pl.BlockSpec(memory_space=pltpu.VMEM),
        name="pack_meta",
    )(starts, table)


def hist_kernel(chunk, tile, local_ref, rows_ref, out_ref, hot):
    bins, total = hot.shape

    @pl.when(pl.program_id(0) == 0)
    def _():
        ids = lax.broadcasted_iota(jnp.int32, (bins, chunk), 0)

        @pl.loop(0, total // chunk)
        def _(k):
            part = pl.ds(pl.multiple_of(k * chunk, chunk), chunk)
            hot[:, part] = (ids == local_ref[:, part]).astype(jnp.bfloat16)

    @pl.loop(0, bins // tile)
    def _(m):
        part = pl.ds(pl.multiple_of(m * tile, tile), tile)
        out_ref[part, :] = jnp.dot(
            hot[part, :], rows_ref[...], preferred_element_type=jnp.float32
        ).astype(out_ref.dtype)


def histogram_of(local, rows, bins, block, dtype):
    total, width = rows.shape
    return pl.pallas_call(
        functools.partial(hist_kernel, math.gcd(total, 128), math.gcd(bins, 256)),
        grid=(width // block,),
        out_shape=jax.ShapeDtypeStruct((bins, width), dtype),
        in_specs=[
            pl.BlockSpec((1, total), lambda j: (0, 0)),
            pl.BlockSpec((total, block), lambda j: (0, j)),
        ],
        out_specs=pl.BlockSpec((bins, block), lambda j: (0, j)),
        scratch_shapes=[pltpu.VMEM((bins, total), jnp.bfloat16)],
        compiler_params=pltpu.CompilerParams(
            vmem_limit_bytes=40 << 20, dimension_semantics=("arbitrary",)
        ),
        cost_estimate=pl.CostEstimate(
            flops=2 * bins * total * width, bytes_accessed=2 * total * width, transcendentals=0
        ),
        name="histogram",
    )(local, rows)


def body(event_bins, event_weights, nominal, background, observed):
    owners = lax.axis_size("bins")
    groups_count = lax.axis_size("params")
    events = event_bins.shape[0]
    width_g = event_weights.shape[1]
    bins_dev = background.shape[0]
    capacity = 3 * events // (2 * owners)
    slot = -(-capacity // ALIGN) * ALIGN + ALIGN
    chunks = 2 if width_g % 512 == 0 else 1
    width = width_g // chunks
    block = math.gcd(width, 256)

    destination = event_bins // bins_dev
    targets = jnp.arange(owners, dtype=jnp.int32)
    before = jnp.sum((destination[None, :] < targets[:, None]).astype(jnp.int32), axis=1)
    starts = jnp.minimum(before // ALIGN, (events - slot) // ALIGN)

    table = jnp.stack([event_bins.astype(jnp.float32), nominal.astype(jnp.float32)])
    table = jnp.concatenate([table, jnp.zeros((6, events), jnp.float32)], axis=0)
    meta = pack_meta(starts, table, slot, bins_dev)
    got_meta = lax.all_to_all(meta, "bins", split_axis=0, concat_axis=0, tiled=True)
    local = got_meta[:, 0].astype(jnp.int32).reshape(1, owners * slot)
    got_nominal = got_meta[:, 1].astype(jnp.bfloat16).reshape(owners * slot, 1)
    got_nominal = jnp.broadcast_to(got_nominal, (owners * slot, 128))
    nominal_sum = histogram_of(local, got_nominal, bins_dev, 128, jnp.float32)[:, 0]
    yields = background + nominal_sum
    curvature = observed / (yields * yields)

    parts = []
    for c in range(chunks):
        packed = pack(starts, event_weights, slot, c * width, width)
        got = lax.all_to_all(packed, "bins", split_axis=0, concat_axis=0, tiled=True)
        got = got.reshape(owners * slot, width)
        parts.append(histogram_of(local, got, bins_dev, block, jnp.bfloat16))
    templates = jnp.concatenate(parts, axis=1)
    weighted = (curvature[:, None] * templates.astype(jnp.float32)).astype(jnp.bfloat16)
    pieces = [templates]
    for shift_by in range(1, groups_count // 2 + 1):
        shifted = [from_behind(part, "params", -shift_by) for part in parts]
        pieces.append(jnp.concatenate(shifted, axis=1))
    partners = jnp.concatenate(pieces, axis=1)
    dims = (((0,), (0,)), ((), ()))
    full = lax.dot_general(weighted, partners, dims, preferred_element_type=jnp.float32)
    full = full.astype(jnp.bfloat16)
    shares = full.reshape(owners, width_g // owners, full.shape[1])
    got = lax.all_to_all(shares, "bins", split_axis=0, concat_axis=0, tiled=True)
    summed = jnp.sum(got.astype(jnp.float32), axis=0)
    return summed * (1.0 / (bins_dev * owners))


def solution(mesh):
    in_specs = (P("bins"), P("bins", "params"), P("bins"), P("bins"), P("bins"))
    out_specs = P(("params", "bins"), None)
    return jax.shard_map(body, mesh=mesh, in_specs=in_specs, out_specs=out_specs, check_vma=False)
```

```python
import functools
import math

import jax
import jax.numpy as jnp
from jax import lax
from jax.experimental import pallas as pl
from jax.experimental.pallas import tpu as pltpu
from jax.sharding import PartitionSpec as P

ALIGN = 8
MESH = pl.DeviceIdType.MESH


def from_behind(value, axis, steps):
    count = lax.axis_size(axis)
    pairs = [(source, (source + steps) % count) for source in range(count)]
    return lax.ppermute(value, axis, pairs)


def pack_kernel(owners, slot, first, width, starts_ref, rows_ref, out_ref, held, in_sems, out_sems):
    def fetch(o):
        start = pl.multiple_of(starts_ref[o] * ALIGN, ALIGN)
        return pltpu.make_async_copy(
            rows_ref.at[pl.ds(start, slot), pl.ds(first, width)], held.at[o], in_sems.at[o]
        )

    def store(o):
        return pltpu.make_async_copy(held.at[o], out_ref.at[o], out_sems.at[o])

    @pl.loop(0, owners)
    def _(o):
        fetch(o).start()

    @pl.loop(0, owners)
    def _(o):
        fetch(o).wait()
        store(o).start()

    @pl.loop(0, owners)
    def _(o):
        store(o).wait()


def pack(starts, rows, slot, first, width):
    owners = starts.shape[0]
    return pl.pallas_call(
        functools.partial(pack_kernel, owners, slot, first, width),
        out_shape=jax.ShapeDtypeStruct((owners, slot, width), rows.dtype),
        in_specs=[
            pl.BlockSpec(memory_space=pltpu.SMEM),
            pl.BlockSpec(memory_space=pl.ANY),
        ],
        out_specs=pl.BlockSpec(memory_space=pl.ANY),
        scratch_shapes=[
            pltpu.VMEM((owners, slot, width), rows.dtype),
            pltpu.SemaphoreType.DMA((owners,)),
            pltpu.SemaphoreType.DMA((owners,)),
        ],
        compiler_params=pltpu.CompilerParams(vmem_limit_bytes=32 << 20),
        cost_estimate=pl.CostEstimate(
            flops=0, bytes_accessed=4 * owners * slot * width, transcendentals=0
        ),
        name="pack",
    )(starts, rows)


def meta_kernel(bins_dev, starts_ref, table_ref, out_ref):
    owners, _, slot = out_ref.shape
    events = table_ref.shape[1]
    table = table_ref[...]

    @pl.loop(0, owners)
    def _(o):
        start = starts_ref[o] * ALIGN
        turned = pltpu.roll(table, lax.rem(events - start, events), axis=1)[:, :slot]
        bins = turned[0:1] - (o * bins_dev).astype(jnp.float32)
        inside = (bins >= 0) & (bins < bins_dev)
        out_ref[o, 0:1, :] = jnp.where(inside, bins, -1.0)
        out_ref[o, 1:2, :] = turned[1:2]


def pack_meta(starts, table, slot, bins_dev):
    owners = starts.shape[0]
    return pl.pallas_call(
        functools.partial(meta_kernel, bins_dev),
        out_shape=jax.ShapeDtypeStruct((owners, 2, slot), jnp.float32),
        in_specs=[
            pl.BlockSpec(memory_space=pltpu.SMEM),
            pl.BlockSpec(memory_space=pltpu.VMEM),
        ],
        out_specs=pl.BlockSpec(memory_space=pltpu.VMEM),
        name="pack_meta",
    )(starts, table)


def hist_kernel(chunk, tile, local_ref, rows_ref, out_ref, hot):
    bins, total = hot.shape

    @pl.when(pl.program_id(0) == 0)
    def _():
        ids = lax.broadcasted_iota(jnp.int32, (bins, chunk), 0)

        @pl.loop(0, total // chunk)
        def _(k):
            part = pl.ds(pl.multiple_of(k * chunk, chunk), chunk)
            hot[:, part] = (ids == local_ref[:, part]).astype(jnp.bfloat16)

    @pl.loop(0, bins // tile)
    def _(m):
        part = pl.ds(pl.multiple_of(m * tile, tile), tile)
        out_ref[part, :] = jnp.dot(
            hot[part, :], rows_ref[...], preferred_element_type=jnp.float32
        ).astype(out_ref.dtype)


def histogram_of(local, rows, bins, block, dtype):
    total, width = rows.shape
    return pl.pallas_call(
        functools.partial(hist_kernel, math.gcd(total, 128), math.gcd(bins, 256)),
        grid=(width // block,),
        out_shape=jax.ShapeDtypeStruct((bins, width), dtype),
        in_specs=[
            pl.BlockSpec((1, total), lambda j: (0, 0)),
            pl.BlockSpec((total, block), lambda j: (0, j)),
        ],
        out_specs=pl.BlockSpec((bins, block), lambda j: (0, j)),
        scratch_shapes=[pltpu.VMEM((bins, total), jnp.bfloat16)],
        compiler_params=pltpu.CompilerParams(
            vmem_limit_bytes=40 << 20, dimension_semantics=("arbitrary",)
        ),
        cost_estimate=pl.CostEstimate(
            flops=2 * bins * total * width, bytes_accessed=2 * total * width, transcendentals=0
        ),
        name="histogram",
    )(local, rows)


def reduce_kernel(
    piece, shares_ref, out_ref, own, got_near, sums, got_far,
    own_sem, near_send, near_recv, far_send, far_recv,
):
    far, near, rows, _ = shares_ref.shape
    me = lax.axis_index("bins")
    f, n = me // near, lax.rem(me, near)

    def near_peer(d):
        return lax.rem(n + d, near)

    def far_peer(d):
        return lax.rem(f + d, far)

    barrier = pltpu.get_barrier_semaphore()
    for d in range(1, near):
        pl.semaphore_signal(
            barrier, inc=1, device_id={"bins": f * near + near_peer(d)}, device_id_type=MESH
        )
    for d in range(1, far):
        pl.semaphore_signal(
            barrier, inc=1, device_id={"bins": far_peer(d) * near + n}, device_id_type=MESH
        )
    pl.semaphore_wait(barrier, near + far - 2)

    def part_of(c):
        return pl.ds(pl.multiple_of(c * piece, piece), piece)

    def near_copy(d, c):
        return pltpu.make_async_remote_copy(
            src_ref=shares_ref.at[:, near_peer(d), part_of(c), :],
            dst_ref=got_near.at[d - 1, :, part_of(c), :],
            send_sem=near_send.at[d - 1, c],
            recv_sem=near_recv.at[d - 1, c],
            device_id={"bins": f * near + near_peer(d)},
            device_id_type=MESH,
        )

    def far_copy(d, c):
        return pltpu.make_async_remote_copy(
            src_ref=sums.at[far_peer(d), part_of(c), :],
            dst_ref=got_far.at[d - 1, part_of(c), :],
            send_sem=far_send.at[d - 1, c],
            recv_sem=far_recv.at[d - 1, c],
            device_id={"bins": far_peer(d) * near + n},
            device_id_type=MESH,
        )

    own_copy = pltpu.make_async_copy(shares_ref.at[:, n], own, own_sem)
    own_copy.start()
    pieces = rows // piece

    @pl.loop(0, pieces)
    def _(c):
        for d in range(1, near):
            near_copy(d, c).start()

    own_copy.wait()

    @pl.loop(0, pieces)
    def _(c):
        part = part_of(c)
        for d in range(1, near):
            near_copy(d, c).wait_recv()

        @pl.loop(0, far)
        def _(k):
            total = own[k, part, :].astype(jnp.float32)
            for d in range(1, near):
                total += got_near[d - 1, k, part, :].astype(jnp.float32)
            sums[k, part, :] = total

        for d in range(1, far):
            far_copy(d, c).start()

    @pl.loop(0, pieces)
    def _(c):
        part = part_of(c)
        for d in range(1, far):
            far_copy(d, c).wait_recv()
        total = sums[f, part, :]
        for d in range(1, far):
            total += got_far[d - 1, part, :]
        out_ref[part, :] = total
        for d in range(1, near):
            near_copy(d, c).wait_send()
        for d in range(1, far):
            far_copy(d, c).wait_send()


def reduce_shares(shares):
    owners, rows, cols = shares.shape
    near = math.isqrt(owners)
    while owners % near:
        near -= 1
    far = owners // near
    piece = 16 if rows % 16 == 0 else rows
    pieces = rows // piece
    return pl.pallas_call(
        functools.partial(reduce_kernel, piece),
        out_shape=jax.ShapeDtypeStruct((rows, cols), jnp.float32),
        in_specs=[pl.BlockSpec(memory_space=pl.ANY)],
        out_specs=pl.BlockSpec(memory_space=pltpu.VMEM),
        scratch_shapes=[
            pltpu.VMEM((far, rows, cols), shares.dtype),
            pltpu.VMEM((near - 1, far, rows, cols), shares.dtype),
            pltpu.VMEM((far, rows, cols), jnp.float32),
            pltpu.VMEM((far - 1, rows, cols), jnp.float32),
            pltpu.SemaphoreType.DMA,
            pltpu.SemaphoreType.DMA((near - 1, pieces)),
            pltpu.SemaphoreType.DMA((near - 1, pieces)),
            pltpu.SemaphoreType.DMA((far - 1, pieces)),
            pltpu.SemaphoreType.DMA((far - 1, pieces)),
        ],
        compiler_params=pltpu.CompilerParams(
            collective_id=1, has_side_effects=True, vmem_limit_bytes=40 << 20
        ),
        name="reduce_shares",
    )(shares.reshape(far, near, rows, cols))


def body(event_bins, event_weights, nominal, background, observed):
    owners = lax.axis_size("bins")
    groups_count = lax.axis_size("params")
    events = event_bins.shape[0]
    width_g = event_weights.shape[1]
    bins_dev = background.shape[0]
    capacity = 3 * events // (2 * owners)
    slot = -(-capacity // ALIGN) * ALIGN + ALIGN
    chunks = 2 if width_g % 512 == 0 else 1
    width = width_g // chunks
    block = math.gcd(width, 256)

    destination = event_bins // bins_dev
    targets = jnp.arange(owners, dtype=jnp.int32)
    before = jnp.sum((destination[None, :] < targets[:, None]).astype(jnp.int32), axis=1)
    starts = jnp.minimum(before // ALIGN, (events - slot) // ALIGN)

    table = jnp.stack([event_bins.astype(jnp.float32), nominal.astype(jnp.float32)])
    table = jnp.concatenate([table, jnp.zeros((6, events), jnp.float32)], axis=0)
    meta = pack_meta(starts, table, slot, bins_dev)
    got_meta = lax.all_to_all(meta, "bins", split_axis=0, concat_axis=0, tiled=True)
    local = got_meta[:, 0].astype(jnp.int32).reshape(1, owners * slot)
    got_nominal = got_meta[:, 1].astype(jnp.bfloat16).reshape(owners * slot, 1)
    got_nominal = jnp.broadcast_to(got_nominal, (owners * slot, 128))
    nominal_sum = histogram_of(local, got_nominal, bins_dev, 128, jnp.float32)[:, 0]
    yields = background + nominal_sum
    curvature = observed / (yields * yields)

    parts = []
    for c in range(chunks):
        packed = pack(starts, event_weights, slot, c * width, width)
        got = lax.all_to_all(packed, "bins", split_axis=0, concat_axis=0, tiled=True)
        got = got.reshape(owners * slot, width)
        parts.append(histogram_of(local, got, bins_dev, block, jnp.bfloat16))
    templates = jnp.concatenate(parts, axis=1)
    weighted = (curvature[:, None] * templates.astype(jnp.float32)).astype(jnp.bfloat16)
    pieces = [templates]
    for shift_by in range(1, groups_count // 2 + 1):
        shifted = [from_behind(part, "params", -shift_by) for part in parts]
        pieces.append(jnp.concatenate(shifted, axis=1))
    partners = jnp.concatenate(pieces, axis=1)
    dims = (((0,), (0,)), ((), ()))
    full = lax.dot_general(weighted, partners, dims, preferred_element_type=jnp.float32)
    full = full.astype(jnp.bfloat16)
    shares = full.reshape(owners, width_g // owners, full.shape[1])
    summed = reduce_shares(shares)
    return summed * (1.0 / (bins_dev * owners))


def solution(mesh):
    in_specs = (P("bins"), P("bins", "params"), P("bins"), P("bins"), P("bins"))
    out_specs = P(("params", "bins"), None)
    return jax.shard_map(body, mesh=mesh, in_specs=in_specs, out_specs=out_specs, check_vma=False)
```

```python
import functools
import math

import jax
import jax.numpy as jnp
from jax import lax
from jax.experimental import pallas as pl
from jax.experimental.pallas import tpu as pltpu
from jax.sharding import PartitionSpec as P

ALIGN = 8
MESH = pl.DeviceIdType.MESH


def from_behind(value, axis, steps):
    count = lax.axis_size(axis)
    pairs = [(source, (source + steps) % count) for source in range(count)]
    return lax.ppermute(value, axis, pairs)


def pack_kernel(owners, slot, first, width, starts_ref, rows_ref, out_ref, held, in_sems, out_sems):
    def fetch(o):
        start = pl.multiple_of(starts_ref[o] * ALIGN, ALIGN)
        return pltpu.make_async_copy(
            rows_ref.at[pl.ds(start, slot), pl.ds(first, width)], held.at[o], in_sems.at[o]
        )

    def store(o):
        return pltpu.make_async_copy(held.at[o], out_ref.at[o], out_sems.at[o])

    @pl.loop(0, owners)
    def _(o):
        fetch(o).start()

    @pl.loop(0, owners)
    def _(o):
        fetch(o).wait()
        store(o).start()

    @pl.loop(0, owners)
    def _(o):
        store(o).wait()


def pack(starts, rows, slot, first, width):
    owners = starts.shape[0]
    return pl.pallas_call(
        functools.partial(pack_kernel, owners, slot, first, width),
        out_shape=jax.ShapeDtypeStruct((owners, slot, width), rows.dtype),
        in_specs=[
            pl.BlockSpec(memory_space=pltpu.SMEM),
            pl.BlockSpec(memory_space=pl.ANY),
        ],
        out_specs=pl.BlockSpec(memory_space=pl.ANY),
        scratch_shapes=[
            pltpu.VMEM((owners, slot, width), rows.dtype),
            pltpu.SemaphoreType.DMA((owners,)),
            pltpu.SemaphoreType.DMA((owners,)),
        ],
        compiler_params=pltpu.CompilerParams(vmem_limit_bytes=56 << 20),
        cost_estimate=pl.CostEstimate(
            flops=0, bytes_accessed=4 * owners * slot * width, transcendentals=0
        ),
        name="pack",
    )(starts, rows)


def meta_kernel(bins_dev, starts_ref, table_ref, out_ref):
    owners, _, slot = out_ref.shape
    events = table_ref.shape[1]
    table = table_ref[...]

    @pl.loop(0, owners)
    def _(o):
        start = starts_ref[o] * ALIGN
        turned = pltpu.roll(table, lax.rem(events - start, events), axis=1)[:, :slot]
        bins = turned[0:1] - (o * bins_dev).astype(jnp.float32)
        inside = (bins >= 0) & (bins < bins_dev)
        out_ref[o, 0:1, :] = jnp.where(inside, bins, -1.0)
        out_ref[o, 1:2, :] = turned[1:2]


def pack_meta(starts, table, slot, bins_dev):
    owners = starts.shape[0]
    return pl.pallas_call(
        functools.partial(meta_kernel, bins_dev),
        out_shape=jax.ShapeDtypeStruct((owners, 2, slot), jnp.float32),
        in_specs=[
            pl.BlockSpec(memory_space=pltpu.SMEM),
            pl.BlockSpec(memory_space=pltpu.VMEM),
        ],
        out_specs=pl.BlockSpec(memory_space=pltpu.VMEM),
        name="pack_meta",
    )(starts, table)


def gather_kernel(
    tile, block, meta_ref, packed_ref, out_ref, nominal_ref, total, own, held,
    own_sem, send_sems, recv_sems,
):
    owners, slot, width = packed_ref.shape
    bins = total.shape[0]
    me = lax.axis_index("bins")

    barrier = pltpu.get_barrier_semaphore()

    @pl.loop(1, owners)
    def _(d):
        pl.semaphore_signal(
            barrier, inc=1, device_id={"bins": lax.rem(me + d, owners)}, device_id_type=MESH
        )

    pl.semaphore_wait(barrier, owners - 1)

    def offset(i):
        return owners // 2 + ((i + 1) // 2) * (1 - 2 * lax.rem(i, 2))

    def copy_of(i):
        target = lax.rem(me + offset(i), owners)
        return pltpu.make_async_remote_copy(
            src_ref=packed_ref.at[target],
            dst_ref=held.at[i],
            send_sem=send_sems.at[i],
            recv_sem=recv_sems.at[i],
            device_id={"bins": target},
            device_id_type=MESH,
        )

    @pl.loop(0, owners - 1)
    def _(i):
        copy_of(i).start()

    own_copy = pltpu.make_async_copy(packed_ref.at[me], own, own_sem)
    own_copy.start()
    own_copy.wait()

    def add(source, rows, first):
        @pl.loop(0, bins // tile)
        def _(m):
            base = pl.multiple_of(m * tile, tile)
            part = pl.ds(base, tile)
            ids = (lax.broadcasted_iota(jnp.int32, (tile, slot), 0) + base).astype(jnp.float32)
            same = ids == meta_ref[source, 0:1, :]
            hot = same.astype(jnp.bfloat16)
            picked = jnp.where(same, meta_ref[source, 1:2, :], 0.0)
            sums = jnp.sum(picked, axis=1, keepdims=True)
            nominal_ref[part, :] = sums if first else nominal_ref[part, :] + sums
            for j in range(width // block):
                cols = pl.ds(j * block, block)
                value = jnp.dot(hot, rows[:, cols], preferred_element_type=jnp.float32)
                total[part, cols] = value if first else total[part, cols] + value

    add(me, own, True)

    @pl.loop(0, owners - 1)
    def _(i):
        copy_of(i).wait_recv()
        add(lax.rem(me - offset(i) + owners, owners), held.at[i], False)

    @pl.loop(0, bins // tile)
    def _(m):
        part = pl.ds(pl.multiple_of(m * tile, tile), tile)
        out_ref[part, :] = total[part, :].astype(out_ref.dtype)

    @pl.loop(0, owners - 1)
    def _(i):
        copy_of(i).wait_send()


def gather_histogram(meta, packed, bins):
    owners, slot, width = packed.shape
    vmem = pl.BlockSpec(memory_space=pltpu.VMEM)
    return pl.pallas_call(
        functools.partial(gather_kernel, math.gcd(bins, 256), math.gcd(width, 512)),
        out_shape=(
            jax.ShapeDtypeStruct((bins, width), jnp.bfloat16),
            jax.ShapeDtypeStruct((bins, 1), jnp.float32),
        ),
        in_specs=[vmem, pl.BlockSpec(memory_space=pl.ANY)],
        out_specs=(vmem, vmem),
        scratch_shapes=[
            pltpu.VMEM((bins, width), jnp.float32),
            pltpu.VMEM((slot, width), packed.dtype),
            pltpu.VMEM((owners - 1, slot, width), packed.dtype),
            pltpu.SemaphoreType.DMA,
            pltpu.SemaphoreType.DMA((owners - 1,)),
            pltpu.SemaphoreType.DMA((owners - 1,)),
        ],
        compiler_params=pltpu.CompilerParams(
            collective_id=2, has_side_effects=True, vmem_limit_bytes=56 << 20
        ),
        name="gather_histogram",
    )(meta, packed)


def reduce_kernel(
    piece, shares_ref, out_ref, own, got_near, sums, got_far,
    own_sem, near_send, near_recv, far_send, far_recv,
):
    far, near, rows, _ = shares_ref.shape
    me = lax.axis_index("bins")
    f, n = me // near, lax.rem(me, near)

    def near_peer(d):
        return lax.rem(n + d, near)

    def far_peer(d):
        return lax.rem(f + d, far)

    barrier = pltpu.get_barrier_semaphore()
    for d in range(1, near):
        pl.semaphore_signal(
            barrier, inc=1, device_id={"bins": f * near + near_peer(d)}, device_id_type=MESH
        )
    for d in range(1, far):
        pl.semaphore_signal(
            barrier, inc=1, device_id={"bins": far_peer(d) * near + n}, device_id_type=MESH
        )
    pl.semaphore_wait(barrier, near + far - 2)

    def part_of(c):
        return pl.ds(pl.multiple_of(c * piece, piece), piece)

    def near_copy(d, c):
        return pltpu.make_async_remote_copy(
            src_ref=shares_ref.at[:, near_peer(d), part_of(c), :],
            dst_ref=got_near.at[d - 1, :, part_of(c), :],
            send_sem=near_send.at[d - 1, c],
            recv_sem=near_recv.at[d - 1, c],
            device_id={"bins": f * near + near_peer(d)},
            device_id_type=MESH,
        )

    def far_copy(d, c):
        return pltpu.make_async_remote_copy(
            src_ref=sums.at[far_peer(d), part_of(c), :],
            dst_ref=got_far.at[d - 1, part_of(c), :],
            send_sem=far_send.at[d - 1, c],
            recv_sem=far_recv.at[d - 1, c],
            device_id={"bins": far_peer(d) * near + n},
            device_id_type=MESH,
        )

    own_copy = pltpu.make_async_copy(shares_ref.at[:, n], own, own_sem)
    own_copy.start()
    pieces = rows // piece

    @pl.loop(0, pieces)
    def _(c):
        for d in range(1, near):
            near_copy(d, c).start()

    own_copy.wait()

    @pl.loop(0, pieces)
    def _(c):
        part = part_of(c)
        for d in range(1, near):
            near_copy(d, c).wait_recv()

        @pl.loop(0, far)
        def _(k):
            total = own[k, part, :].astype(jnp.float32)
            for d in range(1, near):
                total += got_near[d - 1, k, part, :].astype(jnp.float32)
            sums[k, part, :] = total

        for d in range(1, far):
            far_copy(d, c).start()

    @pl.loop(0, pieces)
    def _(c):
        part = part_of(c)
        for d in range(1, far):
            far_copy(d, c).wait_recv()
        total = sums[f, part, :]
        for d in range(1, far):
            total += got_far[d - 1, part, :]
        out_ref[part, :] = total
        for d in range(1, near):
            near_copy(d, c).wait_send()
        for d in range(1, far):
            far_copy(d, c).wait_send()


def reduce_shares(shares):
    owners, rows, cols = shares.shape
    near = math.isqrt(owners)
    while owners % near:
        near -= 1
    far = owners // near
    piece = 16 if rows % 16 == 0 else rows
    pieces = rows // piece
    return pl.pallas_call(
        functools.partial(reduce_kernel, piece),
        out_shape=jax.ShapeDtypeStruct((rows, cols), jnp.float32),
        in_specs=[pl.BlockSpec(memory_space=pl.ANY)],
        out_specs=pl.BlockSpec(memory_space=pltpu.VMEM),
        scratch_shapes=[
            pltpu.VMEM((far, rows, cols), shares.dtype),
            pltpu.VMEM((near - 1, far, rows, cols), shares.dtype),
            pltpu.VMEM((far, rows, cols), jnp.float32),
            pltpu.VMEM((far - 1, rows, cols), jnp.float32),
            pltpu.SemaphoreType.DMA,
            pltpu.SemaphoreType.DMA((near - 1, pieces)),
            pltpu.SemaphoreType.DMA((near - 1, pieces)),
            pltpu.SemaphoreType.DMA((far - 1, pieces)),
            pltpu.SemaphoreType.DMA((far - 1, pieces)),
        ],
        compiler_params=pltpu.CompilerParams(
            collective_id=1, has_side_effects=True, vmem_limit_bytes=56 << 20
        ),
        name="reduce_shares",
    )(shares.reshape(far, near, rows, cols))


def body(event_bins, event_weights, nominal, background, observed):
    owners = lax.axis_size("bins")
    groups_count = lax.axis_size("params")
    events = event_bins.shape[0]
    width_g = event_weights.shape[1]
    bins_dev = background.shape[0]
    capacity = 3 * events // (2 * owners)
    slot = -(-capacity // ALIGN) * ALIGN + ALIGN
    destination = event_bins // bins_dev
    targets = jnp.arange(owners, dtype=jnp.int32)
    before = jnp.sum((destination[None, :] < targets[:, None]).astype(jnp.int32), axis=1)
    starts = jnp.minimum(before // ALIGN, (events - slot) // ALIGN)

    table = jnp.stack([event_bins.astype(jnp.float32), nominal.astype(jnp.float32)])
    table = jnp.concatenate([table, jnp.zeros((6, events), jnp.float32)], axis=0)
    meta = pack_meta(starts, table, slot, bins_dev)
    got_meta = lax.all_to_all(meta, "bins", split_axis=0, concat_axis=0, tiled=True)
    packed = pack(starts, event_weights, slot, 0, width_g)
    templates, nominal_sum = gather_histogram(got_meta, packed, bins_dev)
    yields = background + nominal_sum[:, 0]
    curvature = observed / (yields * yields)
    weighted = (curvature[:, None] * templates.astype(jnp.float32)).astype(jnp.bfloat16)
    pieces = [templates]
    for shift_by in range(1, groups_count // 2 + 1):
        pieces.append(from_behind(templates, "params", -shift_by))
    partners = jnp.concatenate(pieces, axis=1)
    dims = (((0,), (0,)), ((), ()))
    full = lax.dot_general(weighted, partners, dims, preferred_element_type=jnp.float32)
    full = full.astype(jnp.bfloat16)
    shares = full.reshape(owners, width_g // owners, full.shape[1])
    summed = reduce_shares(shares)
    return summed * (1.0 / (bins_dev * owners))


def solution(mesh):
    in_specs = (P("bins"), P("bins", "params"), P("bins"), P("bins"), P("bins"))
    out_specs = P(("params", "bins"), None)
    return jax.shard_map(body, mesh=mesh, in_specs=in_specs, out_specs=out_specs, check_vma=False)
```

```python
import functools
import math

import jax
import jax.numpy as jnp
from jax import lax
from jax.experimental import pallas as pl
from jax.experimental.pallas import tpu as pltpu
from jax.sharding import PartitionSpec as P

ALIGN = 8
MESH = pl.DeviceIdType.MESH


def from_behind(value, axis, steps):
    count = lax.axis_size(axis)
    pairs = [(source, (source + steps) % count) for source in range(count)]
    return lax.ppermute(value, axis, pairs)


def pack_kernel(owners, slot, first, width, starts_ref, rows_ref, out_ref, held, in_sems, out_sems):
    def fetch(o):
        start = pl.multiple_of(starts_ref[o] * ALIGN, ALIGN)
        return pltpu.make_async_copy(
            rows_ref.at[pl.ds(start, slot), pl.ds(first, width)], held.at[o], in_sems.at[o]
        )

    def store(o):
        return pltpu.make_async_copy(held.at[o], out_ref.at[o], out_sems.at[o])

    @pl.loop(0, owners)
    def _(o):
        fetch(o).start()

    @pl.loop(0, owners)
    def _(o):
        fetch(o).wait()
        store(o).start()

    @pl.loop(0, owners)
    def _(o):
        store(o).wait()


def pack(starts, rows, slot, first, width):
    owners = starts.shape[0]
    return pl.pallas_call(
        functools.partial(pack_kernel, owners, slot, first, width),
        out_shape=jax.ShapeDtypeStruct((owners, slot, width), rows.dtype),
        in_specs=[
            pl.BlockSpec(memory_space=pltpu.SMEM),
            pl.BlockSpec(memory_space=pl.ANY),
        ],
        out_specs=pl.BlockSpec(memory_space=pl.ANY),
        scratch_shapes=[
            pltpu.VMEM((owners, slot, width), rows.dtype),
            pltpu.SemaphoreType.DMA((owners,)),
            pltpu.SemaphoreType.DMA((owners,)),
        ],
        compiler_params=pltpu.CompilerParams(vmem_limit_bytes=56 << 20),
        cost_estimate=pl.CostEstimate(
            flops=0, bytes_accessed=4 * owners * slot * width, transcendentals=0
        ),
        name="pack",
    )(starts, rows)


def meta_kernel(bins_dev, starts_ref, table_ref, out_ref):
    owners, _, slot = out_ref.shape
    events = table_ref.shape[1]
    table = table_ref[...]

    @pl.loop(0, owners)
    def _(o):
        start = starts_ref[o] * ALIGN
        turned = pltpu.roll(table, lax.rem(events - start, events), axis=1)[:, :slot]
        bins = turned[0:1] - (o * bins_dev).astype(jnp.float32)
        inside = (bins >= 0) & (bins < bins_dev)
        out_ref[o, 0:1, :] = jnp.where(inside, bins, -1.0)
        out_ref[o, 1:2, :] = turned[1:2]


def pack_meta(starts, table, slot, bins_dev):
    owners = starts.shape[0]
    return pl.pallas_call(
        functools.partial(meta_kernel, bins_dev),
        out_shape=jax.ShapeDtypeStruct((owners, 2, slot), jnp.float32),
        in_specs=[
            pl.BlockSpec(memory_space=pltpu.SMEM),
            pl.BlockSpec(memory_space=pltpu.VMEM),
        ],
        out_specs=pl.BlockSpec(memory_space=pltpu.VMEM),
        name="pack_meta",
    )(starts, table)


def hist_kernel(chunk, tile, local_ref, rows_ref, out_ref, hot):
    bins, total = hot.shape

    @pl.when(pl.program_id(0) == 0)
    def _():
        ids = lax.broadcasted_iota(jnp.int32, (bins, chunk), 0)

        @pl.loop(0, total // chunk)
        def _(k):
            part = pl.ds(pl.multiple_of(k * chunk, chunk), chunk)
            hot[:, part] = (ids == local_ref[:, part]).astype(jnp.bfloat16)

    @pl.loop(0, bins // tile)
    def _(m):
        part = pl.ds(pl.multiple_of(m * tile, tile), tile)
        out_ref[part, :] = jnp.dot(
            hot[part, :], rows_ref[...], preferred_element_type=jnp.float32
        ).astype(out_ref.dtype)


def histogram_of(local, rows, bins, block, dtype):
    total, width = rows.shape
    return pl.pallas_call(
        functools.partial(hist_kernel, math.gcd(total, 128), math.gcd(bins, 256)),
        grid=(width // block,),
        out_shape=jax.ShapeDtypeStruct((bins, width), dtype),
        in_specs=[
            pl.BlockSpec((1, total), lambda j: (0, 0)),
            pl.BlockSpec((total, block), lambda j: (0, j)),
        ],
        out_specs=pl.BlockSpec((bins, block), lambda j: (0, j)),
        scratch_shapes=[pltpu.VMEM((bins, total), jnp.bfloat16)],
        compiler_params=pltpu.CompilerParams(
            vmem_limit_bytes=56 << 20, dimension_semantics=("arbitrary",)
        ),
        cost_estimate=pl.CostEstimate(
            flops=2 * bins * total * width, bytes_accessed=2 * total * width, transcendentals=0
        ),
        name="histogram",
    )(local, rows)


def reduce_kernel(
    piece, shares_ref, out_ref, own, got_near, sums, got_far,
    own_sem, near_send, near_recv, far_send, far_recv,
):
    far, near, rows, _ = shares_ref.shape
    me = lax.axis_index("bins")
    f, n = me // near, lax.rem(me, near)

    def near_peer(d):
        return lax.rem(n + d, near)

    def far_peer(d):
        return lax.rem(f + d, far)

    barrier = pltpu.get_barrier_semaphore()
    for d in range(1, near):
        pl.semaphore_signal(
            barrier, inc=1, device_id={"bins": f * near + near_peer(d)}, device_id_type=MESH
        )
    for d in range(1, far):
        pl.semaphore_signal(
            barrier, inc=1, device_id={"bins": far_peer(d) * near + n}, device_id_type=MESH
        )
    pl.semaphore_wait(barrier, near + far - 2)

    def part_of(c):
        return pl.ds(pl.multiple_of(c * piece, piece), piece)

    def near_copy(d, c):
        return pltpu.make_async_remote_copy(
            src_ref=shares_ref.at[:, near_peer(d), part_of(c), :],
            dst_ref=got_near.at[d - 1, :, part_of(c), :],
            send_sem=near_send.at[d - 1, c],
            recv_sem=near_recv.at[d - 1, c],
            device_id={"bins": f * near + near_peer(d)},
            device_id_type=MESH,
        )

    def far_copy(d, c):
        return pltpu.make_async_remote_copy(
            src_ref=sums.at[far_peer(d), part_of(c), :],
            dst_ref=got_far.at[d - 1, part_of(c), :],
            send_sem=far_send.at[d - 1, c],
            recv_sem=far_recv.at[d - 1, c],
            device_id={"bins": far_peer(d) * near + n},
            device_id_type=MESH,
        )

    own_copy = pltpu.make_async_copy(shares_ref.at[:, n], own, own_sem)
    own_copy.start()
    pieces = rows // piece

    @pl.loop(0, pieces)
    def _(c):
        for d in range(1, near):
            near_copy(d, c).start()

    own_copy.wait()

    @pl.loop(0, pieces)
    def _(c):
        part = part_of(c)
        for d in range(1, near):
            near_copy(d, c).wait_recv()

        @pl.loop(0, far)
        def _(k):
            total = own[k, part, :].astype(jnp.float32)
            for d in range(1, near):
                total += got_near[d - 1, k, part, :].astype(jnp.float32)
            sums[k, part, :] = total

        for d in range(1, far):
            far_copy(d, c).start()

    @pl.loop(0, pieces)
    def _(c):
        part = part_of(c)
        for d in range(1, far):
            far_copy(d, c).wait_recv()
        total = sums[f, part, :]
        for d in range(1, far):
            total += got_far[d - 1, part, :]
        out_ref[part, :] = total
        for d in range(1, near):
            near_copy(d, c).wait_send()
        for d in range(1, far):
            far_copy(d, c).wait_send()


def reduce_shares(shares):
    owners, rows, cols = shares.shape
    near = math.isqrt(owners)
    while owners % near:
        near -= 1
    far = owners // near
    piece = 16 if rows % 16 == 0 else rows
    pieces = rows // piece
    return pl.pallas_call(
        functools.partial(reduce_kernel, piece),
        out_shape=jax.ShapeDtypeStruct((rows, cols), jnp.float32),
        in_specs=[pl.BlockSpec(memory_space=pl.ANY)],
        out_specs=pl.BlockSpec(memory_space=pltpu.VMEM),
        scratch_shapes=[
            pltpu.VMEM((far, rows, cols), shares.dtype),
            pltpu.VMEM((near - 1, far, rows, cols), shares.dtype),
            pltpu.VMEM((far, rows, cols), jnp.float32),
            pltpu.VMEM((far - 1, rows, cols), jnp.float32),
            pltpu.SemaphoreType.DMA,
            pltpu.SemaphoreType.DMA((near - 1, pieces)),
            pltpu.SemaphoreType.DMA((near - 1, pieces)),
            pltpu.SemaphoreType.DMA((far - 1, pieces)),
            pltpu.SemaphoreType.DMA((far - 1, pieces)),
        ],
        compiler_params=pltpu.CompilerParams(
            collective_id=1, has_side_effects=True, vmem_limit_bytes=56 << 20
        ),
        name="reduce_shares",
    )(shares.reshape(far, near, rows, cols))


def body(event_bins, event_weights, nominal, background, observed):
    owners = lax.axis_size("bins")
    groups_count = lax.axis_size("params")
    events = event_bins.shape[0]
    width_g = event_weights.shape[1]
    bins_dev = background.shape[0]
    capacity = 3 * events // (2 * owners)
    slot = -(-capacity // ALIGN) * ALIGN + ALIGN
    chunks = 1
    width = width_g // chunks
    block = math.gcd(width, 256)

    destination = event_bins // bins_dev
    targets = jnp.arange(owners, dtype=jnp.int32)
    before = jnp.sum((destination[None, :] < targets[:, None]).astype(jnp.int32), axis=1)
    starts = jnp.minimum(before // ALIGN, (events - slot) // ALIGN)

    table = jnp.stack([event_bins.astype(jnp.float32), nominal.astype(jnp.float32)])
    table = jnp.concatenate([table, jnp.zeros((6, events), jnp.float32)], axis=0)
    meta = pack_meta(starts, table, slot, bins_dev)
    got_meta = lax.all_to_all(meta, "bins", split_axis=0, concat_axis=0, tiled=True)
    local = got_meta[:, 0].astype(jnp.int32).reshape(1, owners * slot)
    got_nominal = got_meta[:, 1].astype(jnp.bfloat16).reshape(owners * slot, 1)
    got_nominal = jnp.broadcast_to(got_nominal, (owners * slot, 128))
    nominal_sum = histogram_of(local, got_nominal, bins_dev, 128, jnp.float32)[:, 0]
    parts = []
    for c in range(chunks):
        packed = pack(starts, event_weights, slot, c * width, width)
        got = lax.all_to_all(packed, "bins", split_axis=0, concat_axis=0, tiled=True)
        got, nominal_sum = lax.optimization_barrier((got, nominal_sum))
        got = got.reshape(owners * slot, width)
        parts.append(histogram_of(local, got, bins_dev, block, jnp.bfloat16))
    yields = background + nominal_sum
    curvature = observed / (yields * yields)
    templates = jnp.concatenate(parts, axis=1)
    weighted = (curvature[:, None] * templates.astype(jnp.float32)).astype(jnp.bfloat16)
    pieces = [templates]
    for shift_by in range(1, groups_count // 2 + 1):
        shifted = [from_behind(part, "params", -shift_by) for part in parts]
        pieces.append(jnp.concatenate(shifted, axis=1))
    partners = jnp.concatenate(pieces, axis=1)
    dims = (((0,), (0,)), ((), ()))
    full = lax.dot_general(weighted, partners, dims, preferred_element_type=jnp.float32)
    full = full.astype(jnp.bfloat16)
    shares = full.reshape(owners, width_g // owners, full.shape[1])
    summed = reduce_shares(shares)
    return summed * (1.0 / (bins_dev * owners))


def solution(mesh):
    in_specs = (P("bins"), P("bins", "params"), P("bins"), P("bins"), P("bins"))
    out_specs = P(("params", "bins"), None)
    return jax.shard_map(body, mesh=mesh, in_specs=in_specs, out_specs=out_specs, check_vma=False)
```
